32 devices in a mesh: seq: 8 (over z, y), dp: 4 (over x, core).
Axes of the slice: x: 2, y: 2, z: 4, core: 2. Of those that a mesh axis runs over, the one named last changes fastest.
Arguments:
- embeddings: bfloat16 [24, 768, 768], P('dp', 'seq'), may hold values from -6 to 6
- kernels: bfloat16 [2, 3, 768, 768], replicated, may hold values from -0.125 to 0.125
- cotangent: bfloat16 [24, 768, 768], P('dp', 'seq'), may hold values from -6 to 6
Outputs:
- block_output: bfloat16 [24, 768, 768], P('dp', 'seq')
- input_grad: bfloat16 [24, 768, 768], P('dp', 'seq')
- kernel_grad: float32 [2, 3, 768, 768], P(None, None, 'dp', 'seq')
The draws below stay inside these ranges and needn't reach their ends.
All inputs are finite; a program needn't handle non-finite values.
Results may differ from the reference program's by a relative error of at most 0.0054.
Values may be sent and summed in bfloat16 or wider, within the bound.
No kernel may reach another device: no remote copies, remote signals or barrier semaphores. Data moves between devices by JAX's collectives and lax.ppermute only.
A program may use at most 128 MiB of HBM per device.

```python
import math
from functools import partial
import jax
import jax.numpy as jnp
from jax import lax

C = 768
LAYERS = 2
FIRST_DILATION = 8
LEN = 768
BATCH = 24


def with_spikes(drawn, stream_key, source, target, shards_of, factor):
    def block_of(dim):
        return (jnp.arange(drawn.shape[dim]) // (drawn.shape[dim] // shards_of)).reshape((-1,) + (1,) * (drawn.ndim - 1 - dim))

    first = jax.random.permutation(stream_key, shards_of)[block_of(target)]
    second = (block_of(target) + shards_of // 2) % shards_of
    return jnp.where((block_of(source) == first) | (block_of(source) == second), factor * drawn, drawn)


def level_of(rng, dims, split, least, top_value):
    def one(dim, shards_of):
        heights = jax.random.uniform(jax.random.fold_in(jax.random.fold_in(rng, 6), dim), (shards_of,), jnp.float32, least / len(split), top_value / len(split))
        return jnp.repeat(jnp.exp(heights), dims[dim] // shards_of).reshape((-1,) + (1,) * (len(dims) - dim - 1))

    loudness = one(*split[0])
    for cut in split[1:]:
        loudness = loudness * one(*cut)
    return loudness


def centred(own_key, extent, deviation, reach, shards=(), held_as=jnp.bfloat16):
    factor_of = level_of(own_key, extent, shards, -0.22, 0.18) if shards else 1.0
    drawn = jax.random.normal(own_key, extent, jnp.float32) * deviation * factor_of
    return jnp.minimum(jnp.maximum(drawn, -reach), reach).astype(held_as)


def bell_draw_with(key, dims, deviation, most, pieces, heavy, held_as=jnp.bfloat16):
    entries = deviation * jax.random.normal(key, dims, jnp.float32)
    if pieces:
        entries = entries * level_of(key, dims, pieces, -0.22, 0.18)
    return jnp.clip(with_spikes(entries, jax.random.fold_in(key, 3), *heavy), -most, most).astype(held_as)


def setup_inputs(seed: int = 0) -> dict:
    arg_keys = jax.random.split(jax.random.key(seed), 4)
    embeddings = centred(arg_keys[0], (BATCH, LEN, C), 1.0, 6.0, ((0, 4), (1, 8)))
    kernels = centred(arg_keys[1], (LAYERS, 3, C, C), (3 * C) ** -0.5, 0.125)
    cotangent = bell_draw_with(arg_keys[2], (BATCH, LEN, C), 1.0, 6.0, ((0, 4), (1, 8)), (1, 2, 8, 2.0))
    return {"embeddings": embeddings, "kernels": kernels, "cotangent": cotangent}


def normed(hidden):
    wide = hidden.astype(jnp.float32)
    recip = lax.rsqrt(lax.optimization_barrier(jnp.mean(wide * wide, axis=-1, keepdims=True)) + 1e-05)
    return (wide * recip, recip, wide)

def dilated(padded, weight, dilation_rate, output_length, offsets):
    batches = padded.shape[0]
    channels = padded.shape[2]
    summed = jnp.zeros((batches * output_length, weight.shape[2]), jnp.float32)
    for kernel_tap in range(3):
        start = offsets[kernel_tap] * dilation_rate
        window = padded[:, start:start + output_length, :].reshape(batches * output_length, channels)
        summed = summed + jnp.dot(window, weight[kernel_tap], preferred_element_type=jnp.float32)
    return summed.reshape(batches, output_length, weight.shape[2])

def tap_grads(padded, upstream_gradient, dilation_rate, output_length):
    channels = padded.shape[2]
    flat_up = upstream_gradient.reshape(-1, upstream_gradient.shape[2])
    piece_parts = []
    for kernel_tap in range(3):
        start = kernel_tap * dilation_rate
        window = padded[:, start:start + output_length, :].reshape(-1, channels)
        piece_parts.append(lax.dot_general(window, flat_up, (((0,), (0,)), ((), ())), preferred_element_type=jnp.float32))
    return jnp.stack(piece_parts)

def reference(embeddings, kernels, cotangent):
    current = embeddings
    saved = []
    for layer_index in range(LAYERS):
        dilation_rate = FIRST_DILATION * 2 ** layer_index
        normal_activation, recip, wide = normed(current)
        active = jax.nn.gelu(normal_activation, approximate=True).astype(jnp.bfloat16)
        padded = jnp.pad(active, ((0, 0), (dilation_rate, dilation_rate), (0, 0)))
        saved.append((current, padded))
        mixed = dilated(padded, kernels[layer_index], dilation_rate, LEN, (0, 1, 2))
        current = (current.astype(jnp.float32) + mixed).astype(jnp.bfloat16)
    factor = 1.0 / math.sqrt(BATCH * LEN)
    grad_h = cotangent.astype(jnp.float32)
    grads = [None] * LAYERS
    for layer_index in reversed(range(LAYERS)):
        dilation_rate = FIRST_DILATION * 2 ** layer_index
        hidden, padded = saved[layer_index]
        upstream_gradient = grad_h.astype(jnp.bfloat16)
        grads[layer_index] = tap_grads(padded, upstream_gradient, dilation_rate, LEN) * factor
        padded_up = jnp.pad(upstream_gradient, ((0, 0), (dilation_rate, dilation_rate), (0, 0)))
        swapped = jnp.swapaxes(kernels[layer_index], 1, 2)
        back_conv = dilated(padded_up, swapped, dilation_rate, LEN, (2, 1, 0))
        normal_activation, recip, wide = normed(hidden)
        primal, pullback = jax.vjp(partial(jax.nn.gelu, approximate=True), normal_activation)
        through = pullback(back_conv)[0]
        inner = lax.optimization_barrier(jnp.mean(through * wide, axis=-1, keepdims=True))
        grad_h = grad_h + recip * through - wide * recip * recip * recip * inner
    return (current, grad_h.astype(jnp.bfloat16), jnp.stack(grads))
```

```python
import math
from functools import partial

import jax
import jax.numpy as jnp
from jax import lax
from jax.experimental import pallas as pl
from jax.experimental.pallas import tpu as pltpu
from jax.sharding import PartitionSpec as P

FIRST_DILATION = 8
F32 = jnp.float32
BF16 = jnp.bfloat16
VMEM = pl.BlockSpec(memory_space=pltpu.VMEM)
SMEM = pl.BlockSpec(memory_space=pltpu.SMEM)
VMEM_LIMIT = 28 * 2**20
ROOT = math.sqrt(2.0 / math.pi)
CUBE = 0.044715


def kernel_call(body, args, outs, flops=0, scalars=None, scratch=()):
    moved = sum(a.size * a.dtype.itemsize for a in args)
    moved += sum(math.prod(o.shape) * o.dtype.itemsize for o in outs)
    specs = [VMEM] * len(args)
    if scalars is not None:
        args, specs = [scalars, *args], [SMEM, *specs]
    return pl.pallas_call(
        body,
        out_shape=tuple(outs),
        in_specs=specs,
        out_specs=tuple(VMEM for _ in outs),
        scratch_shapes=list(scratch),
        compiler_params=pltpu.CompilerParams(vmem_limit_bytes=VMEM_LIMIT),
        cost_estimate=pl.CostEstimate(flops=flops, bytes_accessed=moved, transcendentals=0),
    )(*args)


def shape(dims, dtype=BF16):
    return jax.ShapeDtypeStruct(tuple(dims), dtype)


def normed(hidden):
    wide = hidden.astype(F32)
    recip = lax.rsqrt(jnp.mean(wide * wide, axis=-1, keepdims=True) + 1e-05)
    return wide * recip, recip, wide


def gelu(v):
    return 0.5 * v * (1.0 + jnp.tanh(ROOT * (v + CUBE * (v * v * v))))


def gelu_slope(v):
    square = v * v
    t = jnp.tanh(ROOT * v * (1.0 + CUBE * square))
    return 0.5 * (1.0 + t) + 0.5 * v * (1.0 - t * t) * (ROOT * (1.0 + 3.0 * CUBE * square))


def flat(cells):
    return cells.reshape(-1, cells.shape[-1])


def dot(a, b):
    return jnp.dot(a, b, preferred_element_type=F32)


def dot_nt(a, b):
    return lax.dot_general(a, b, (((1,), (1,)), ((), ())), preferred_element_type=F32)


def dot_tn(a, b):
    return lax.dot_general(a, b, (((0,), (0,)), ((), ())), preferred_element_type=F32)


def windows(above, own, below):
    width, rows = above.shape[1], own.shape[1]
    before = jnp.concatenate([above, own[:, : rows - width]], axis=1)
    after = jnp.concatenate([own[:, width:], below], axis=1)
    return flat(before), flat(own), flat(after)


def halves(cells, parity):
    q = cells.shape[-1] // 4
    even = jnp.concatenate([cells[..., :q], cells[..., 2 * q : 3 * q]], axis=-1)
    odd = jnp.concatenate([cells[..., q : 2 * q], cells[..., 3 * q :]], axis=-1)
    first = parity == 0
    return jnp.where(first, even, odd), jnp.where(first, odd, even)


def by_low_bit(cells, count):
    w = cells.shape[-1] // count
    order = [*range(0, count, 2), *range(1, count, 2)]
    return jnp.concatenate([cells[..., j * w : (j + 1) * w] for j in order], axis=-1)


def first_body(h_ref, w_ref, s_ref, z_ref):
    act, _, _ = normed(h_ref[...])
    s = gelu(act)
    edge = jnp.zeros((s.shape[0], FIRST_DILATION, s.shape[2]), F32)
    before, own, after = (v.astype(BF16) for v in windows(edge, s, edge))
    s_ref[...] = own.reshape(s_ref.shape)
    z = dot(own, w_ref[1]) + dot(before, w_ref[0]) + dot(after, w_ref[2])
    z_ref[...] = z.reshape(z_ref.shape)


def second_body(where_ref, z_ref, h_ref, s_ref, up_ref, down_ref, w_ref, h1_ref, s1_ref, keep_ref, send_ref, kx_ref, sx_ref):
    width = up_ref.shape[1]
    rows = h_ref.shape[1]
    parity = where_ref[0]
    above = gelu(normed(up_ref[...])[0])
    below = gelu(normed(down_ref[...])[0])
    s = s_ref[...]
    ext = jnp.concatenate([above, s.astype(F32), below], axis=1).astype(BF16)
    kept, sent = halves(ext, parity)
    kx_ref[...] = kept
    sx_ref[...] = sent
    add_top = dot(flat(above).astype(BF16), w_ref[0]).reshape(above.shape)
    add_low = dot(flat(below).astype(BF16), w_ref[2]).reshape(below.shape)
    z = z_ref[...]
    z = jnp.concatenate([z[:, :width] + add_top, z[:, width : rows - width], z[:, rows - width :] + add_low], axis=1)
    h1 = (h_ref[...].astype(F32) + z).astype(BF16)
    h1_ref[...] = h1
    s1 = gelu(normed(h1)[0]).astype(BF16)
    s1_ref[...] = s1
    kept, sent = halves(s1, parity)
    keep_ref[...] = kept
    send_ref[...] = sent


def extend_body(count, up_ref, own_ref, down_ref, out_ref):
    ext = jnp.concatenate([up_ref[...], own_ref[...], down_ref[...]], axis=1)
    out_ref[...] = by_low_bit(ext, count)


def back_conv(q_ref, up_ref, down_ref, w_ref, h_ref, g):
    wide_q = q_ref[...].astype(F32)
    before, own, after = windows(up_ref[...].astype(F32), wide_q, down_ref[...].astype(F32))
    e = dot_nt(own.astype(BF16), w_ref[1])
    e += dot_nt(after.astype(BF16), w_ref[0])
    e += dot_nt(before.astype(BF16), w_ref[2])
    act, recip, wide = normed(h_ref[...])
    through = e.reshape(act.shape) * gelu_slope(act)
    inner = jnp.mean(through * wide, axis=-1, keepdims=True)
    return g + recip * through - wide * (recip * recip * recip * inner)


def back_body(count, q_ref, up_ref, down_ref, w_ref, h_ref, g_ref, out_ref, mixed_ref):
    g = back_conv(q_ref, up_ref, down_ref, w_ref, h_ref, q_ref[...].astype(F32))
    g_ref[...] = g
    q = g.astype(BF16)
    out_ref[...] = q
    mixed_ref[...] = by_low_bit(q, count)


def last_back_body(q_ref, up_ref, down_ref, w_ref, h_ref, g_ref, out_ref):
    out_ref[...] = back_conv(q_ref, up_ref, down_ref, w_ref, h_ref, g_ref[...]).astype(BF16)


def last_body(s_ref, up_ref, down_ref, w_ref, h_ref, out_ref):
    before, own, after = windows(up_ref[...], s_ref[...], down_ref[...])
    z = dot(before, w_ref[0]) + dot(own, w_ref[1]) + dot(after, w_ref[2])
    out_ref[...] = (h_ref[...].astype(F32) + z.reshape(h_ref.shape)).astype(BF16)


def grad_body(taps_of_s, where_ref, s_ref, s2_ref, q_ref, q2_ref, keep_ref, send_ref, d_ref):
    rows = s_ref.shape[1] if not taps_of_s else q_ref.shape[1]
    wide = q_ref.shape[2] // 2
    tall = s_ref.shape[2] // 2

    def cut(ref, start):
        return flat(ref[:, start : start + rows, :])

    def pair(a_ref, b_ref, start):
        return jnp.concatenate([cut(a_ref, start), cut(b_ref, start)], axis=0)

    if taps_of_s:
        step = (s_ref.shape[1] - rows) // 2
        q = pair(q_ref, q2_ref, 0)
    else:
        step = (q_ref.shape[1] - rows) // 2
        s = pair(s_ref, s2_ref, 0)
    for tap in range(3):
        if taps_of_s:
            s = pair(s_ref, s2_ref, tap * step)
        else:
            q = pair(q_ref, q2_ref, (2 - tap) * step)
        d = dot_tn(s, q)
        for i in range(2):
            for j in range(2):
                d_ref[tap, i, j] = d[i * tall : (i + 1) * tall, j * wide : (j + 1) * wide]
    first = where_ref[0] == 0
    x, y = where_ref[1], where_ref[2]
    for i in range(2):
        kx, ky = jnp.where(first, x, i), jnp.where(first, i, y)
        gx, gy = jnp.where(first, 1 - x, i), jnp.where(first, i, 1 - y)
        for tap in range(3):
            keep_ref[i, tap] = d_ref[tap, kx, ky]
            send_ref[i, tap] = d_ref[tap, gx, gy].astype(BF16)


def weave_body(count, keep_ref, got_ref, out_ref):
    total = flat(keep_ref[...] + got_ref[...].astype(F32))
    w, r = total.shape[1] // count, total.shape[0] // count
    for block in range(count):
        out_ref[block] = jnp.concatenate(
            [total[g * r : (g + 1) * r, block * w : (block + 1) * w] for g in range(count)], axis=1
        )


def unweave_body(count, factor, keep_ref, got_ref, out_ref):
    total = (keep_ref[...] + got_ref[...].astype(F32)) * factor
    w = total.shape[1] // count
    rows = jnp.concatenate([total[:, g * w : (g + 1) * w] for g in range(count)], axis=0)
    out_ref[...] = rows.reshape(out_ref.shape)


def pick(cells, bit, axis):
    return lax.dynamic_index_in_dim(cells, bit, axis, keepdims=False)


def per_device(embeddings, kernels, cotangent):
    batches, rows, channels = embeddings.shape
    seqs, dps = lax.axis_size("seq"), lax.axis_size("dp")
    axes = ("seq", "dp")
    near, far = FIRST_DILATION, 2 * FIRST_DILATION
    seq, dp = lax.axis_index("seq"), lax.axis_index("dp")
    where = jnp.stack([dp % 2, (dp // 2) % 2, seq % 2]).astype(jnp.int32)
    tokens = batches * rows
    conv_flops = 6 * tokens * channels * channels
    own = (batches, rows, channels)

    up = partial(lax.ppermute, axis_name="seq", perm=[(i, i + 1) for i in range(seqs - 1)])
    down = partial(lax.ppermute, axis_name="seq", perm=[(i + 1, i) for i in range(seqs - 1)])
    swap = partial(lax.ppermute, axis_name="dp", perm=[(i, i ^ 1) for i in range(dps)])

    def crossed(first):
        pairs = []
        for s in range(seqs):
            for d in range(dps):
                along_dp = (d % 2 == 0) == first
                t = (s, d ^ 2) if along_dp else (s ^ 1, d)
                pairs.append((s * dps + d, t[0] * dps + t[1]))
        return partial(lax.ppermute, axis_name=axes, perm=pairs)

    def along(bit):
        return partial(lax.ppermute, axis_name="seq", perm=[(i, i ^ bit) for i in range(seqs)])

    h_up, h_down = up(embeddings[:, rows - near :]), down(embeddings[:, :near])
    q_up, q_down = up(cotangent[:, rows - far :]), down(cotangent[:, :far])

    s0, z0 = kernel_call(
        first_body, [embeddings, kernels[0]], [shape(own), shape(own, F32)], conv_flops
    )
    (qx,) = kernel_call(
        partial(extend_body, seqs), [q_up, cotangent, q_down], [shape((batches, rows + 2 * far, channels))]
    )
    qx2 = swap(qx)
    half = channels // 2
    h1, s1, s1_keep, s1_send, s0_keep, s0_send = kernel_call(
        second_body,
        [z0, embeddings, s0, h_up, h_down, kernels[0]],
        [
            shape(own),
            shape(own),
            shape((batches, rows, half)),
            shape((batches, rows, half)),
            shape((batches, rows + 2 * near, half)),
            shape((batches, rows + 2 * near, half)),
        ],
        conv_flops // 10,
        where,
    )
    s1_other, s0_other = swap(s1_send), swap(s0_send)

    blocks = (2, 3, half // 2, half)

    def grad(taps_of_s, s, s2, q, q2):
        return kernel_call(
            partial(grad_body, taps_of_s),
            [s, s2, q, q2],
            [shape(blocks, F32), shape(blocks)],
            conv_flops,
            where,
            [pltpu.VMEM((3, 2, 2, half // 2, half), F32)],
        )

    count = seqs // 2
    strip = 3 * (half // 2) // count
    woven = strip % 16 == 0
    turn = jnp.where(dp % 2 == 0, seq % 2, (dp // 2) % 2)
    factor = 1.0 / math.sqrt(batches * dps * rows * seqs)

    def reduced(keep, send):
        got = crossed(True)(send)
        total = keep + got.astype(F32)
        keep, send = pick(total, turn, 0), pick(total, 1 - turn, 0).astype(BF16)
        got = crossed(False)(send)
        if woven:
            (total,) = kernel_call(
                partial(weave_body, count), [keep, got], [shape((count, strip, half), F32)]
            )
        else:
            total = (keep + got.astype(F32)).reshape(count, strip, count, half // count)
            total = total.transpose(2, 1, 0, 3).reshape(count, strip, half)
        bit = 1
        while 2 * bit < seqs:
            mine = (seq // (2 * bit)) % 2
            pairs = total.reshape(total.shape[0] // 2, 2, strip, half)
            keep, send = pick(pairs, mine, 1), pick(pairs, 1 - mine, 1).astype(BF16)
            got = along(2 * bit)(send)
            bit *= 2
            if 2 * bit < seqs:
                total = keep + got.astype(F32)
        final = (3, half // 2, half // count)
        if woven:
            (out,) = kernel_call(partial(unweave_body, count, factor), [keep[0], got[0]], [shape(final, F32)])
            return out
        total = (keep[0] + got[0].astype(F32)) * factor
        return total.reshape(strip, count, half // count).transpose(1, 0, 2).reshape(final)

    keep1, send1 = grad(False, s1_keep, s1_other, qx, qx2)
    grad1 = reduced(keep1, send1)

    g1, q0, q0_mixed = kernel_call(
        partial(back_body, seqs),
        [cotangent, q_up, q_down, kernels[1], h1],
        [shape(own, F32), shape(own), shape(own)],
        conv_flops,
    )
    q0_other = swap(q0_mixed)
    keep0, send0 = grad(True, s0_keep, s0_other, q0_mixed, q0_other)
    grad0 = reduced(keep0, send0)

    s1_up, s1_down = up(s1[:, rows - far :]), down(s1[:, :far])
    q0_up, q0_down = up(q0[:, rows - near :]), down(q0[:, :near])
    (out,) = kernel_call(last_body, [s1, s1_up, s1_down, kernels[1], h1], [shape(own)], conv_flops)
    (grad_in,) = kernel_call(
        last_back_body, [q0, q0_up, q0_down, kernels[0], embeddings, g1], [shape(own)], conv_flops
    )
    return out, grad_in, jnp.stack([grad0, grad1])


def solution(mesh):
    placed = (P("dp", "seq", None), P(), P("dp", "seq", None))
    return jax.shard_map(
        per_device,
        mesh=mesh,
        in_specs=placed,
        out_specs=(P("dp", "seq", None), P("dp", "seq", None), P(None, None, "dp", "seq")),
        check_vma=False,
    )
```

```python
import math
from functools import partial

import jax
import jax.numpy as jnp
from jax import lax
from jax.experimental import pallas as pl
from jax.experimental.pallas import tpu as pltpu
from jax.sharding import PartitionSpec as P

FIRST_DILATION = 8
F32 = jnp.float32
BF16 = jnp.bfloat16
VMEM = pl.BlockSpec(memory_space=pltpu.VMEM)
VMEM_LIMIT = 20 * 2**20
ROOT = math.sqrt(2.0 / math.pi)
CUBE = 0.044715


def kernel_call(body, args, outs, flops=0):
    moved = sum(a.size * a.dtype.itemsize for a in args)
    moved += sum(math.prod(o.shape) * o.dtype.itemsize for o in outs)
    return pl.pallas_call(
        body,
        out_shape=tuple(outs),
        in_specs=[VMEM] * len(args),
        out_specs=tuple(VMEM for _ in outs),
        compiler_params=pltpu.CompilerParams(vmem_limit_bytes=VMEM_LIMIT),
        cost_estimate=pl.CostEstimate(flops=flops, bytes_accessed=moved, transcendentals=0),
    )(*args)


def shape(dims, dtype=BF16):
    return jax.ShapeDtypeStruct(tuple(dims), dtype)


def bit_of(axis, bit):
    return (lax.axis_index(axis) >> bit) & 1


def normed(hidden):
    wide = hidden.astype(F32)
    recip = lax.rsqrt(jnp.mean(wide * wide, axis=-1, keepdims=True) + 1e-05)
    return wide * recip, recip, wide


def gelu(v):
    return 0.5 * v * (1.0 + jnp.tanh(ROOT * (v + CUBE * (v * v * v))))


def gelu_slope(v):
    square = v * v
    t = jnp.tanh(ROOT * v * (1.0 + CUBE * square))
    return 0.5 * (1.0 + t) + 0.5 * v * (1.0 - t * t) * (ROOT * (1.0 + 3.0 * CUBE * square))


def flat(cells):
    return cells.reshape(-1, cells.shape[-1])


def dot(a, b):
    return jnp.dot(a, b, preferred_element_type=F32)


def dot_nt(a, b):
    return lax.dot_general(a, b, (((1,), (1,)), ((), ())), preferred_element_type=F32)


def dot_tn(a, b):
    return lax.dot_general(a, b, (((0,), (0,)), ((), ())), preferred_element_type=F32)


def windows(above, own, below):
    width, rows = above.shape[1], own.shape[1]
    before = jnp.concatenate([above, own[:, : rows - width]], axis=1)
    after = jnp.concatenate([own[:, width:], below], axis=1)
    return flat(before), flat(own), flat(after)


def quarters(cells, parity, turn):
    q = cells.shape[-1] // 4
    a, b, c, d = (cells[..., i * q : (i + 1) * q] for i in range(4))
    even, odd = jnp.concatenate([a, c], axis=-1), jnp.concatenate([b, d], axis=-1)
    even_back, odd_back = jnp.concatenate([c, a], axis=-1), jnp.concatenate([d, b], axis=-1)
    even, odd = jnp.where(turn == 0, even, even_back), jnp.where(turn == 0, odd, odd_back)
    return jnp.where(parity == 0, even, odd), jnp.where(parity == 0, odd, even)


def by_low_bit(cells, count, turn):
    w = cells.shape[-1] // count
    even = jnp.concatenate([cells[..., j * w : (j + 1) * w] for j in range(0, count, 2)], axis=-1)
    odd = jnp.concatenate([cells[..., j * w : (j + 1) * w] for j in range(1, count, 2)], axis=-1)
    return jnp.concatenate([jnp.where(turn == 0, even, odd), jnp.where(turn == 0, odd, even)], axis=-1)


def store_edges(cells, ref_a, ref_b, at):
    width = cells.shape[1] // 2
    even = bit_of("seq", 0) == 0
    head, tail = cells[:, :width], cells[:, width:]
    ref_a[:, at : at + width] = jnp.where(even, tail, head)
    ref_b[:, at : at + width] = jnp.where(even, head, tail)


def halos(ref_a, ref_b, at, width):
    even = bit_of("seq", 0) == 0
    a, b = ref_a[:, at : at + width], ref_b[:, at : at + width]
    return jnp.where(even, b, a), jnp.where(even, a, b)


def edge_body(near, far, h_ref, q_ref, a_ref, b_ref):
    rows = h_ref.shape[1]
    q = jnp.concatenate([q_ref[:, :far], q_ref[:, rows - far :]], axis=1)
    h = jnp.concatenate([h_ref[:, :near], h_ref[:, rows - near :]], axis=1)
    store_edges(q, a_ref, b_ref, 0)
    store_edges(h, a_ref, b_ref, far)


def first_body(near, h_ref, w_ref, s_ref, z_ref):
    act, _, _ = normed(h_ref[...])
    s = gelu(act)
    edge = jnp.zeros((s.shape[0], near, s.shape[2]), F32)
    before, own, after = (v.astype(BF16) for v in windows(edge, s, edge))
    s_ref[...] = own.reshape(s_ref.shape)
    z = dot(own, w_ref[0, 1]) + dot(before, w_ref[0, 0]) + dot(after, w_ref[0, 2])
    z_ref[...] = z.reshape(z_ref.shape)


def second_body(near, far, z_ref, h_ref, s_ref, a_ref, b_ref, w_ref, h1_ref, s1_ref, keep_ref, send_ref, kx_ref, sx_ref):
    rows = h_ref.shape[1]
    parity, turn = bit_of("dp", 0), bit_of("dp", 1)
    above, below = halos(a_ref, b_ref, far, near)
    above, below = gelu(normed(above)[0]), gelu(normed(below)[0])
    ext = jnp.concatenate([above, s_ref[...].astype(F32), below], axis=1).astype(BF16)
    kx_ref[...], sx_ref[...] = quarters(ext, parity, turn)
    add_top = dot(flat(above).astype(BF16), w_ref[0, 0]).reshape(above.shape)
    add_low = dot(flat(below).astype(BF16), w_ref[0, 2]).reshape(below.shape)
    z = z_ref[...]
    z = jnp.concatenate([z[:, :near] + add_top, z[:, near : rows - near], z[:, rows - near :] + add_low], axis=1)
    h1 = (h_ref[...].astype(F32) + z).astype(BF16)
    h1_ref[...] = h1
    s1 = gelu(normed(h1)[0]).astype(BF16)
    s1_ref[...] = s1
    keep_ref[...], send_ref[...] = quarters(s1, parity, turn)


def back_conv(layer, dtype, above, below, q, w_ref, h_ref, g):
    before, own, after = windows(above.astype(dtype), q.astype(dtype), below.astype(dtype))
    e = dot_nt(own.astype(BF16), w_ref[layer, 1])
    e += dot_nt(after.astype(BF16), w_ref[layer, 0])
    e += dot_nt(before.astype(BF16), w_ref[layer, 2])
    act, recip, wide = normed(h_ref[...])
    through = e.reshape(act.shape) * gelu_slope(act)
    inner = jnp.mean(through * wide, axis=-1, keepdims=True)
    return g + recip * through - wide * (recip * recip * recip * inner)


def back_body(near, far, count, q_ref, a_ref, b_ref, w_ref, h_ref, s_ref, g_ref, out_ref, mixed_ref, na_ref, nb_ref):
    rows = q_ref.shape[1]
    above, below = halos(a_ref, b_ref, 0, far)
    g = back_conv(1, BF16, above, below, q_ref[...], w_ref, h_ref, q_ref[...].astype(F32))
    g_ref[...] = g
    q = g.astype(BF16)
    out_ref[...] = q
    mixed_ref[...] = by_low_bit(q, count, bit_of("seq", 0))
    s = jnp.concatenate([s_ref[:, :far], s_ref[:, rows - far :]], axis=1)
    store_edges(s, na_ref, nb_ref, 0)
    ends = jnp.concatenate([g[:, :near], g[:, rows - near :]], axis=1).astype(BF16)
    store_edges(ends, na_ref, nb_ref, far)


def last_back_body(near, far, q_ref, a_ref, b_ref, w_ref, h_ref, g_ref, out_ref):
    above, below = halos(a_ref, b_ref, far, near)
    out_ref[...] = back_conv(0, F32, above, below, q_ref[...], w_ref, h_ref, g_ref[...]).astype(BF16)


def last_body(far, s_ref, a_ref, b_ref, w_ref, h_ref, out_ref):
    above, below = halos(a_ref, b_ref, 0, far)
    before, own, after = windows(above, s_ref[...], below)
    z = dot(before, w_ref[1, 0]) + dot(own, w_ref[1, 1]) + dot(after, w_ref[1, 2])
    out_ref[...] = (h_ref[...].astype(F32) + z.reshape(h_ref.shape)).astype(BF16)


def store_grad(tap, d, keep_ref, send_ref):
    tall, wide = d.shape[0] // 2, d.shape[1] // 2
    first = bit_of("dp", 0) == 0
    right, low = d[:tall, wide:], d[tall:, :wide]
    keep_ref[0, tap] = d[:tall, :wide]
    keep_ref[1, tap] = jnp.where(first, right, low)
    send_ref[0, tap] = jnp.where(first, low, right).astype(BF16)
    send_ref[1, tap] = d[tall:, wide:].astype(BF16)


def grad_near_body(s_ref, s2_ref, q_ref, q2_ref, keep_ref, send_ref):
    rows = q_ref.shape[1]
    step = (s_ref.shape[1] - rows) // 2
    q = jnp.concatenate([flat(q_ref[...]), flat(q2_ref[...])], axis=0)
    for tap in range(3):
        cut = slice(tap * step, tap * step + rows)
        s = jnp.concatenate([flat(s_ref[:, cut]), flat(s2_ref[:, cut])], axis=0)
        store_grad(tap, dot_tn(s, q), keep_ref, send_ref)


def grad_far_body(far, count, s_ref, s2_ref, q_ref, q2_ref, a_ref, b_ref, a2_ref, b2_ref, keep_ref, send_ref):
    turn = bit_of("seq", 0)
    s = jnp.concatenate([flat(s_ref[...]), flat(s2_ref[...])], axis=0)
    taps = []
    for own_ref, at_a, at_b in ((q_ref, a_ref, b_ref), (q2_ref, a2_ref, b2_ref)):
        above, below = halos(at_a, at_b, 0, far)
        before, own, after = windows(*(by_low_bit(v, count, turn) for v in (above, own_ref[...], below)))
        taps.append((after, own, before))
    for tap in range(3):
        q = jnp.concatenate([taps[0][tap], taps[1][tap]], axis=0)
        store_grad(tap, dot_tn(s, q), keep_ref, send_ref)


def pass_body(keep_ref, got_ref, send_ref):
    for slot in range(send_ref.shape[0]):
        send_ref[slot] = (keep_ref[2 * slot + 1] + got_ref[2 * slot + 1].astype(F32)).astype(BF16)


def weave_body(count, keep_ref, got_ref, more_ref, out_ref, send_ref, all_ref):
    total = flat(keep_ref[0] + got_ref[0].astype(F32) + more_ref[0].astype(F32))
    w, r = total.shape[1] // count, total.shape[0] // count
    for block in range(count):
        all_ref[block] = jnp.concatenate(
            [total[g * r : (g + 1) * r, block * w : (block + 1) * w] for g in range(count)], axis=1
        )
    mine = lax.axis_index("seq") >> 1
    for slot in range(count // 2):
        out_ref[slot] = all_ref[mine ^ (2 * slot)]
        send_ref[slot] = all_ref[mine ^ (2 * slot + 1)].astype(BF16)


def final_body(count, factor, *refs):
    out_ref = refs[-1]
    for layer in range(out_ref.shape[0]):
        keep_ref, got_ref, more_ref = refs[3 * layer : 3 * layer + 3]
        total = (keep_ref[0] + got_ref[0].astype(F32) + more_ref[0].astype(F32)) * factor
        w = total.shape[1] // count
        rows = jnp.concatenate([total[:, g * w : (g + 1) * w] for g in range(count)], axis=0)
        out_ref[layer] = rows.reshape(out_ref.shape[1:])


def per_device(embeddings, kernels, cotangent):
    batches, rows, channels = embeddings.shape
    seqs, dps = lax.axis_size("seq"), lax.axis_size("dp")
    near, far = FIRST_DILATION, 2 * FIRST_DILATION
    conv_flops = 6 * batches * rows * channels * channels
    half = channels // 2
    own = (batches, rows, channels)
    edges = (batches, near + far, channels)

    def paired(partner):
        pairs = []
        for s in range(seqs):
            for d in range(dps):
                t, e = partner(s, d)
                if 0 <= t < seqs:
                    pairs.append((s * dps + d, t * dps + e))
        return partial(lax.ppermute, axis_name=("seq", "dp"), perm=pairs)

    swap = paired(lambda s, d: (s, d ^ 1))
    to_a = paired(lambda s, d: (s ^ 1, d))
    to_b = paired(lambda s, d: (((s + 1) ^ 1) - 1, d))
    cross_one = paired(lambda s, d: (s, d ^ 2) if d % 2 == 0 else (s ^ 1, d))
    cross_two = paired(lambda s, d: (s ^ 1, d) if d % 2 == 0 else (s, d ^ 2))

    def along(bit):
        return paired(lambda s, d: (s ^ bit, d))

    send_a, send_b = kernel_call(
        partial(edge_body, near, far), [embeddings, cotangent], [shape(edges), shape(edges)]
    )
    got_a, got_b = to_a(send_a), to_b(send_b)
    q1_other = swap(cotangent)
    s0, z0 = kernel_call(
        partial(first_body, near), [embeddings, kernels], [shape(own), shape(own, F32)], conv_flops
    )
    other_a, other_b = swap(got_a), swap(got_b)
    h1, s1, s1_keep, s1_send, s0_keep, s0_send = kernel_call(
        partial(second_body, near, far),
        [z0, embeddings, s0, got_a, got_b, kernels],
        [
            shape(own),
            shape(own),
            shape((batches, rows, half)),
            shape((batches, rows, half)),
            shape((batches, rows + 2 * near, half)),
            shape((batches, rows + 2 * near, half)),
        ],
        conv_flops // 10,
    )
    s1_other, s0_other = swap(s1_send), swap(s0_send)

    blocks = [shape((2, 3, half // 2, half), F32), shape((2, 3, half // 2, half))]
    count = seqs // 2
    strip = 3 * (half // 2) // count
    woven = strip % 16 == 0
    factor = 1.0 / math.sqrt(batches * dps * rows * seqs)

    def passed(keep, got):
        (send,) = kernel_call(pass_body, [keep, got], [shape((keep.shape[0] // 2, *keep.shape[1:]))])
        return send

    def reduced(keep, send):
        got = cross_one(send)
        more = cross_two(passed(keep, got))
        if woven:
            keep, send, _ = kernel_call(
                partial(weave_body, count),
                [keep, got, more],
                [
                    shape((count // 2, strip, half), F32),
                    shape((count // 2, strip, half)),
                    shape((count, strip, half), F32),
                ],
            )
        else:
            total = keep[0] + got[0].astype(F32) + more[0].astype(F32)
            total = total.reshape(count, strip, count, half // count)
            total = total.transpose(2, 1, 0, 3).reshape(count, strip, half)
            total = total[jnp.arange(count) ^ (lax.axis_index("seq") // 2)]
            keep, send = total[0::2], total[1::2].astype(BF16)
        got, bit = along(2)(send), 4
        while 2 * bit < seqs:
            total = keep + got.astype(F32)
            keep, got, bit = total[0::2], along(bit)(total[1::2].astype(BF16)), 2 * bit
        if bit < seqs:
            return keep, got, along(bit)(passed(keep, got))
        return keep, got, jnp.zeros_like(got)

    keep1, send1 = kernel_call(
        partial(grad_far_body, far, seqs),
        [s1_keep, s1_other, cotangent, q1_other, got_a, got_b, other_a, other_b],
        blocks,
        conv_flops,
    )
    parts1 = reduced(keep1, send1)

    g1, q0, q0_mixed, send_a, send_b = kernel_call(
        partial(back_body, near, far, seqs),
        [cotangent, got_a, got_b, kernels, h1, s1],
        [shape(own, F32), shape(own), shape(own), shape(edges), shape(edges)],
        conv_flops,
    )
    q0_other = swap(q0_mixed)
    keep0, send0 = kernel_call(
        grad_near_body, [s0_keep, s0_other, q0_mixed, q0_other], blocks, conv_flops
    )
    parts0 = reduced(keep0, send0)

    got_a, got_b = to_a(send_a), to_b(send_b)
    (out,) = kernel_call(
        partial(last_body, far), [s1, got_a, got_b, kernels, h1], [shape(own)], conv_flops
    )
    (grad_in,) = kernel_call(
        partial(last_back_body, near, far),
        [q0, got_a, got_b, kernels, embeddings, g1],
        [shape(own)],
        conv_flops,
    )
    final = (2, 3, half // 2, half // count)
    if woven:
        (grads,) = kernel_call(
            partial(final_body, count, factor), [*parts0, *parts1], [shape(final, F32)]
        )
        return out, grad_in, grads
    grads = []
    for keep, got, more in (parts0, parts1):
        total = (keep[0] + got[0].astype(F32) + more[0].astype(F32)) * factor
        grads.append(total.reshape(strip, count, half // count).transpose(1, 0, 2).reshape(final[1:]))
    return out, grad_in, jnp.stack(grads)


def solution(mesh):
    placed = (P("dp", "seq", None), P(), P("dp", "seq", None))
    return jax.shard_map(
        per_device,
        mesh=mesh,
        in_specs=placed,
        out_specs=(P("dp", "seq", None), P("dp", "seq", None), P(None, None, "dp", "seq")),
        check_vma=False,
    )
```

```python
import math
from functools import partial

import jax
import jax.numpy as jnp
from jax import lax
from jax.experimental import pallas as pl
from jax.experimental.pallas import tpu as pltpu
from jax.sharding import PartitionSpec as P

FIRST_DILATION = 8
F32 = jnp.float32
BF16 = jnp.bfloat16
VMEM = pl.BlockSpec(memory_space=pltpu.VMEM)
VMEM_LIMIT = 20 * 2**20
ROOT = math.sqrt(2.0 / math.pi)
CUBE = 0.044715


def kernel_call(body, args, outs, flops=0, after=()):
    if after:
        inner, first = body, len(args)
        body = lambda *refs: inner(*refs[:first], *refs[first + len(after) :])
    moved = sum(a.size * a.dtype.itemsize for a in args)
    moved += sum(math.prod(o.shape) * o.dtype.itemsize for o in outs)
    return pl.pallas_call(
        body,
        out_shape=tuple(outs),
        in_specs=[VMEM] * len(args) + [pl.BlockSpec(memory_space=pl.ANY)] * len(after),
        out_specs=tuple(VMEM for _ in outs),
        compiler_params=pltpu.CompilerParams(vmem_limit_bytes=VMEM_LIMIT),
        cost_estimate=pl.CostEstimate(flops=flops, bytes_accessed=moved, transcendentals=0),
    )(*args, *after)


def shape(dims, dtype=BF16):
    return jax.ShapeDtypeStruct(tuple(dims), dtype)


def bit_of(axis, bit):
    return (lax.axis_index(axis) >> bit) & 1


def normed(hidden):
    wide = hidden.astype(F32)
    recip = lax.rsqrt(jnp.mean(wide * wide, axis=-1, keepdims=True) + 1e-05)
    return wide * recip, recip, wide


def gelu(v):
    return 0.5 * v * (1.0 + jnp.tanh(ROOT * (v + CUBE * (v * v * v))))


def gelu_slope(v):
    square = v * v
    t = jnp.tanh(ROOT * v * (1.0 + CUBE * square))
    return 0.5 * (1.0 + t) + 0.5 * v * (1.0 - t * t) * (ROOT * (1.0 + 3.0 * CUBE * square))


def flat(cells):
    return cells.reshape(-1, cells.shape[-1])


def dot(a, b):
    return jnp.dot(a, b, preferred_element_type=F32)


def dot_nt(a, b):
    return lax.dot_general(a, b, (((1,), (1,)), ((), ())), preferred_element_type=F32)


def dot_tn(a, b):
    return lax.dot_general(a, b, (((0,), (0,)), ((), ())), preferred_element_type=F32)


def windows(above, own, below):
    width, rows = above.shape[1], own.shape[1]
    before = jnp.concatenate([above, own[:, : rows - width]], axis=1)
    after = jnp.concatenate([own[:, width:], below], axis=1)
    return flat(before), flat(own), flat(after)


def quarters(cells, parity, turn):
    q = cells.shape[-1] // 4
    a, b, c, d = (cells[..., i * q : (i + 1) * q] for i in range(4))
    even, odd = jnp.concatenate([a, c], axis=-1), jnp.concatenate([b, d], axis=-1)
    even_back, odd_back = jnp.concatenate([c, a], axis=-1), jnp.concatenate([d, b], axis=-1)
    even, odd = jnp.where(turn == 0, even, even_back), jnp.where(turn == 0, odd, odd_back)
    return jnp.where(parity == 0, even, odd), jnp.where(parity == 0, odd, even)


def by_low_bit(cells, count, turn):
    w = cells.shape[-1] // count
    even = jnp.concatenate([cells[..., j * w : (j + 1) * w] for j in range(0, count, 2)], axis=-1)
    odd = jnp.concatenate([cells[..., j * w : (j + 1) * w] for j in range(1, count, 2)], axis=-1)
    return jnp.concatenate([jnp.where(turn == 0, even, odd), jnp.where(turn == 0, odd, even)], axis=-1)


def store_edges(cells, ref_a, ref_b, at):
    width = cells.shape[1] // 2
    even = bit_of("seq", 0) == 0
    head, tail = cells[:, :width], cells[:, width:]
    ref_a[:, at : at + width] = jnp.where(even, tail, head)
    ref_b[:, at : at + width] = jnp.where(even, head, tail)


def halos(ref_a, ref_b, at, width):
    even = bit_of("seq", 0) == 0
    a, b = ref_a[:, at : at + width], ref_b[:, at : at + width]
    return jnp.where(even, b, a), jnp.where(even, a, b)


def edge_body(near, far, h_ref, q_ref, a_ref, b_ref):
    rows = h_ref.shape[1]
    q = jnp.concatenate([q_ref[:, :far], q_ref[:, rows - far :]], axis=1)
    h = jnp.concatenate([h_ref[:, :near], h_ref[:, rows - near :]], axis=1)
    store_edges(q, a_ref, b_ref, 0)
    store_edges(h, a_ref, b_ref, far)


def first_body(near, h_ref, w_ref, s_ref, z_ref):
    act, _, _ = normed(h_ref[...])
    s = gelu(act)
    edge = jnp.zeros((s.shape[0], near, s.shape[2]), F32)
    before, own, after = (v.astype(BF16) for v in windows(edge, s, edge))
    s_ref[...] = own.reshape(s_ref.shape)
    z = dot(own, w_ref[0, 1]) + dot(before, w_ref[0, 0]) + dot(after, w_ref[0, 2])
    z_ref[...] = z.reshape(z_ref.shape)


def second_body(near, far, z_ref, h_ref, s_ref, a_ref, b_ref, w_ref, h1_ref, s1_ref, keep_ref, send_ref, kx_ref, sx_ref, na_ref, nb_ref, ends_ref):
    rows = h_ref.shape[1]
    parity, turn = bit_of("dp", 0), bit_of("dp", 1)
    above, below = halos(a_ref, b_ref, far, near)
    above, below = gelu(normed(above)[0]), gelu(normed(below)[0])
    ext = jnp.concatenate([above, s_ref[...].astype(F32), below], axis=1).astype(BF16)
    ends_ref[:, :far], ends_ref[:, far:] = halos(a_ref, b_ref, 0, far)
    kx_ref[...], sx_ref[...] = quarters(ext, parity, turn)
    add_top = dot(flat(above).astype(BF16), w_ref[0, 0]).reshape(above.shape)
    add_low = dot(flat(below).astype(BF16), w_ref[0, 2]).reshape(below.shape)
    z = z_ref[...]
    z = jnp.concatenate([z[:, :near] + add_top, z[:, near : rows - near], z[:, rows - near :] + add_low], axis=1)
    h1 = (h_ref[...].astype(F32) + z).astype(BF16)
    h1_ref[...] = h1
    s1 = gelu(normed(h1)[0]).astype(BF16)
    s1_ref[...] = s1
    store_edges(jnp.concatenate([s1[:, :far], s1[:, rows - far :]], axis=1), na_ref, nb_ref, 0)
    keep_ref[...], send_ref[...] = quarters(s1, parity, turn)


def back_conv(layer, dtype, above, below, q, w_ref):
    before, own, after = windows(above.astype(dtype), q.astype(dtype), below.astype(dtype))
    e = dot_nt(own.astype(BF16), w_ref[layer, 1])
    e += dot_nt(after.astype(BF16), w_ref[layer, 0])
    return e + dot_nt(before.astype(BF16), w_ref[layer, 2])


def through_norm(e, h_ref, g):
    act, recip, wide = normed(h_ref[...])
    through = e.reshape(act.shape) * gelu_slope(act)
    inner = jnp.mean(through * wide, axis=-1, keepdims=True)
    return g + recip * through - wide * (recip * recip * recip * inner)


def back_inner_body(far, q_ref, w_ref, e_ref):
    edge = jnp.zeros((q_ref.shape[0], far, q_ref.shape[2]), BF16)
    e_ref[...] = back_conv(1, BF16, edge, edge, q_ref[...], w_ref).reshape(e_ref.shape)


def back_body(near, far, count, e_ref, q_ref, a_ref, b_ref, w_ref, h_ref, g_ref, out_ref, mixed_ref, na_ref, nb_ref):
    rows = q_ref.shape[1]
    above, below = halos(a_ref, b_ref, 0, far)
    top = e_ref[:, :far] + dot_nt(flat(above), w_ref[1, 2]).reshape(above.shape)
    low = e_ref[:, rows - far :] + dot_nt(flat(below), w_ref[1, 0]).reshape(below.shape)
    e = jnp.concatenate([top, e_ref[:, far : rows - far], low], axis=1)
    g = through_norm(e, h_ref, q_ref[...].astype(F32))
    g_ref[...] = g
    q = g.astype(BF16)
    out_ref[...] = q
    mixed_ref[...] = by_low_bit(q, count, bit_of("seq", 0))
    ends = jnp.concatenate([g[:, :near], g[:, rows - near :]], axis=1).astype(BF16)
    store_edges(ends, na_ref, nb_ref, 0)


def last_back_body(near, q_ref, a_ref, b_ref, w_ref, h_ref, g_ref, out_ref):
    above, below = halos(a_ref, b_ref, 0, near)
    e = back_conv(0, F32, above, below, q_ref[...], w_ref)
    out_ref[...] = through_norm(e, h_ref, g_ref[...]).astype(BF16)


def last_body(far, s_ref, a_ref, b_ref, w_ref, h_ref, out_ref):
    above, below = halos(a_ref, b_ref, 0, far)
    before, own, after = windows(above, s_ref[...], below)
    z = dot(before, w_ref[1, 0]) + dot(own, w_ref[1, 1]) + dot(after, w_ref[1, 2])
    out_ref[...] = (h_ref[...].astype(F32) + z.reshape(h_ref.shape)).astype(BF16)


def store_grad(tap, d, keep_ref, send_ref):
    tall, wide = d.shape[0] // 2, d.shape[1] // 2
    first = bit_of("dp", 0) == 0
    right, low = d[:tall, wide:], d[tall:, :wide]
    keep_ref[0, tap] = d[:tall, :wide]
    keep_ref[1, tap] = jnp.where(first, right, low)
    send_ref[0, tap] = jnp.where(first, low, right).astype(BF16)
    send_ref[1, tap] = d[tall:, wide:].astype(BF16)


def grad_near_body(s_ref, s2_ref, q_ref, q2_ref, keep_ref, send_ref):
    rows = q_ref.shape[1]
    step = (s_ref.shape[1] - rows) // 2
    q = jnp.concatenate([flat(q_ref[...]), flat(q2_ref[...])], axis=0)
    for tap in range(3):
        cut = slice(tap * step, tap * step + rows)
        s = jnp.concatenate([flat(s_ref[:, cut]), flat(s2_ref[:, cut])], axis=0)
        store_grad(tap, dot_tn(s, q), keep_ref, send_ref)


def grad_far_body(far, count, s_ref, s2_ref, q_ref, q2_ref, ends_ref, ends2_ref, keep_ref, send_ref):
    turn = bit_of("seq", 0)
    s = jnp.concatenate([flat(s_ref[...]), flat(s2_ref[...])], axis=0)
    taps = []
    for own_ref, at_ref in ((q_ref, ends_ref), (q2_ref, ends2_ref)):
        above, below = at_ref[:, :far], at_ref[:, far:]
        before, own, after = windows(*(by_low_bit(v, count, turn) for v in (above, own_ref[...], below)))
        taps.append((after, own, before))
    for tap in range(3):
        q = jnp.concatenate([taps[0][tap], taps[1][tap]], axis=0)
        store_grad(tap, dot_tn(s, q), keep_ref, send_ref)


def pass_body(keep_ref, got_ref, send_ref):
    for slot in range(send_ref.shape[0]):
        send_ref[slot] = (keep_ref[2 * slot + 1] + got_ref[2 * slot + 1].astype(F32)).astype(BF16)


def weave_body(count, keep_ref, got_ref, more_ref, out_ref, send_ref, all_ref):
    total = flat(keep_ref[0] + got_ref[0].astype(F32) + more_ref[0].astype(F32))
    w, r = total.shape[1] // count, total.shape[0] // count
    for block in range(count):
        all_ref[block] = jnp.concatenate(
            [total[g * r : (g + 1) * r, block * w : (block + 1) * w] for g in range(count)], axis=1
        )
    mine = lax.axis_index("seq") >> 1
    for slot in range(count // 2):
        out_ref[slot] = all_ref[mine ^ (2 * slot)]
        send_ref[slot] = all_ref[mine ^ (2 * slot + 1)].astype(BF16)


def final_body(count, factor, *refs):
    out_ref = refs[-1]
    for layer in range(out_ref.shape[0]):
        keep_ref, got_ref, more_ref = refs[3 * layer : 3 * layer + 3]
        total = (keep_ref[0] + got_ref[0].astype(F32) + more_ref[0].astype(F32)) * factor
        w = total.shape[1] // count
        rows = jnp.concatenate([total[:, g * w : (g + 1) * w] for g in range(count)], axis=0)
        out_ref[layer] = rows.reshape(out_ref.shape[1:])


def per_device(embeddings, kernels, cotangent):
    batches, rows, channels = embeddings.shape
    seqs, dps = lax.axis_size("seq"), lax.axis_size("dp")
    near, far = FIRST_DILATION, 2 * FIRST_DILATION
    conv_flops = 6 * batches * rows * channels * channels
    half = channels // 2
    own = (batches, rows, channels)
    edges = (batches, near + far, channels)

    def paired(partner):
        pairs = []
        for s in range(seqs):
            for d in range(dps):
                t, e = partner(s, d)
                if 0 <= t < seqs:
                    pairs.append((s * dps + d, t * dps + e))
        return partial(lax.ppermute, axis_name=("seq", "dp"), perm=pairs)

    swap = paired(lambda s, d: (s, d ^ 1))
    to_a = paired(lambda s, d: (s ^ 1, d))
    to_b = paired(lambda s, d: (((s + 1) ^ 1) - 1, d))
    cross_one = paired(lambda s, d: (s, d ^ 2) if d % 2 == 0 else (s ^ 1, d))
    cross_two = paired(lambda s, d: (s ^ 1, d) if d % 2 == 0 else (s, d ^ 2))

    def along(bit):
        return paired(lambda s, d: (s ^ bit, d))

    send_a, send_b = kernel_call(
        partial(edge_body, near, far), [embeddings, cotangent], [shape(edges), shape(edges)]
    )
    got_a, got_b = to_a(send_a), to_b(send_b)
    q1_other = swap(cotangent)
    s0, z0 = kernel_call(
        partial(first_body, near), [embeddings, kernels], [shape(own), shape(own, F32)], conv_flops
    )
    (e1,) = kernel_call(
        partial(back_inner_body, far), [cotangent, kernels], [shape(own, F32)], conv_flops
    )
    h1, s1, s1_keep, s1_send, s0_keep, s0_send, s1_a, s1_b, ends = kernel_call(
        partial(second_body, near, far),
        [z0, embeddings, s0, got_a, got_b, kernels],
        [
            shape(own),
            shape(own),
            shape((batches, rows, half)),
            shape((batches, rows, half)),
            shape((batches, rows + 2 * near, half)),
            shape((batches, rows + 2 * near, half)),
            shape((batches, far, channels)),
            shape((batches, far, channels)),
            shape((batches, 2 * far, channels)),
        ],
        conv_flops // 10,
        [e1],
    )
    ends_other, s1_other, s0_other = swap(ends), swap(s1_send), swap(s0_send)
    s1_a, s1_b = to_a(s1_a), to_b(s1_b)

    blocks = [shape((2, 3, half // 2, half), F32), shape((2, 3, half // 2, half))]
    count = seqs // 2
    strip = 3 * (half // 2) // count
    woven = strip % 16 == 0
    factor = 1.0 / math.sqrt(batches * dps * rows * seqs)

    def passed(keep, got, after=()):
        sent = shape((keep.shape[0] // 2, *keep.shape[1:]))
        (send,) = kernel_call(pass_body, [keep, got], [sent], after=after)
        return send

    def reduced(keep, got, after=()):
        more = cross_two(passed(keep, got, after))
        if woven:
            keep, send, _ = kernel_call(
                partial(weave_body, count),
                [keep, got, more],
                [
                    shape((count // 2, strip, half), F32),
                    shape((count // 2, strip, half)),
                    shape((count, strip, half), F32),
                ],
            )
        else:
            total = keep[0] + got[0].astype(F32) + more[0].astype(F32)
            total = total.reshape(count, strip, count, half // count)
            total = total.transpose(2, 1, 0, 3).reshape(count, strip, half)
            total = total[jnp.arange(count) ^ (lax.axis_index("seq") // 2)]
            keep, send = total[0::2], total[1::2].astype(BF16)
        got, bit = along(2)(send), 4
        while 2 * bit < seqs:
            total = keep + got.astype(F32)
            keep, got, bit = total[0::2], along(bit)(total[1::2].astype(BF16)), 2 * bit
        if bit < seqs:
            return keep, got, along(bit)(passed(keep, got))
        return keep, got, jnp.zeros_like(got)

    g1, q0, q0_mixed, send_a, send_b = kernel_call(
        partial(back_body, near, far, seqs),
        [e1, cotangent, got_a, got_b, kernels, h1],
        [shape(own, F32), shape(own), shape(own)] + [shape((batches, near, channels))] * 2,
        conv_flops // 10,
    )
    q0_a, q0_b = to_a(send_a), to_b(send_b)
    keep1, send1 = kernel_call(
        partial(grad_far_body, far, seqs),
        [s1_keep, s1_other, cotangent, q1_other, ends, ends_other],
        blocks,
        conv_flops,
        [g1],
    )
    half1 = cross_one(send1)

    q0_other = swap(q0_mixed)
    keep0, send0 = kernel_call(
        grad_near_body, [s0_keep, s0_other, q0_mixed, q0_other], blocks, conv_flops, [s1_a, s1_b]
    )
    half0 = cross_one(send0)
    parts1 = reduced(keep1, half1, [send0])
    parts0 = reduced(keep0, half0, [q0_a, q0_b])

    (out,) = kernel_call(
        partial(last_body, far), [s1, s1_a, s1_b, kernels, h1], [shape(own)], conv_flops
    )
    (grad_in,) = kernel_call(
        partial(last_back_body, near),
        [q0, q0_a, q0_b, kernels, embeddings, g1],
        [shape(own)],
        conv_flops,
    )
    final = (2, 3, half // 2, half // count)
    if woven:
        (grads,) = kernel_call(
            partial(final_body, count, factor), [*parts0, *parts1], [shape(final, F32)]
        )
        return out, grad_in, grads
    grads = []
    for keep, got, more in (parts0, parts1):
        total = (keep[0] + got[0].astype(F32) + more[0].astype(F32)) * factor
        grads.append(total.reshape(strip, count, half // count).transpose(1, 0, 2).reshape(final[1:]))
    return out, grad_in, jnp.stack(grads)


def solution(mesh):
    placed = (P("dp", "seq", None), P(), P("dp", "seq", None))
    return jax.shard_map(
        per_device,
        mesh=mesh,
        in_specs=placed,
        out_specs=(P("dp", "seq", None), P("dp", "seq", None), P(None, None, "dp", "seq")),
        check_vma=False,
    )
```

```python
import math
from functools import partial

import jax
import jax.numpy as jnp
from jax import lax
from jax.experimental import pallas as pl
from jax.experimental.pallas import tpu as pltpu
from jax.sharding import PartitionSpec as P

FIRST_DILATION = 8
F32 = jnp.float32
BF16 = jnp.bfloat16
VMEM = pl.BlockSpec(memory_space=pltpu.VMEM)
VMEM_LIMIT = 20 * 2**20
ROOT = math.sqrt(2.0 / math.pi)
CUBE = 0.044715


def kernel_call(body, args, outs, flops=0, after=()):
    if after:
        inner, first = body, len(args)
        body = lambda *refs: inner(*refs[:first], *refs[first + len(after) :])
    moved = sum(a.size * a.dtype.itemsize for a in args)
    moved += sum(math.prod(o.shape) * o.dtype.itemsize for o in outs)
    return pl.pallas_call(
        body,
        out_shape=tuple(outs),
        in_specs=[VMEM] * len(args) + [pl.BlockSpec(memory_space=pl.ANY)] * len(after),
        out_specs=tuple(VMEM for _ in outs),
        compiler_params=pltpu.CompilerParams(vmem_limit_bytes=VMEM_LIMIT),
        cost_estimate=pl.CostEstimate(flops=flops, bytes_accessed=moved, transcendentals=0),
    )(*args, *after)


def shape(dims, dtype=BF16):
    return jax.ShapeDtypeStruct(tuple(dims), dtype)


def bit_of(axis, bit):
    return (lax.axis_index(axis) >> bit) & 1


def normed(hidden):
    wide = hidden.astype(F32)
    recip = lax.rsqrt(jnp.mean(wide * wide, axis=-1, keepdims=True) + 1e-05)
    return wide * recip, recip, wide


def gelu(v):
    return 0.5 * v * (1.0 + jnp.tanh(ROOT * (v + CUBE * (v * v * v))))


def gelu_slope(v):
    square = v * v
    t = jnp.tanh(ROOT * v * (1.0 + CUBE * square))
    return 0.5 * (1.0 + t) + 0.5 * v * (1.0 - t * t) * (ROOT * (1.0 + 3.0 * CUBE * square))


def flat(cells):
    return cells.reshape(-1, cells.shape[-1])


def dot(a, b):
    return jnp.dot(a, b, preferred_element_type=F32)


def dot_nt(a, b):
    return lax.dot_general(a, b, (((1,), (1,)), ((), ())), preferred_element_type=F32)


def dot_tn(a, b):
    return lax.dot_general(a, b, (((0,), (0,)), ((), ())), preferred_element_type=F32)


def windows(above, own, below):
    width, rows = above.shape[1], own.shape[1]
    before = jnp.concatenate([above, own[:, : rows - width]], axis=1)
    after = jnp.concatenate([own[:, width:], below], axis=1)
    return flat(before), flat(own), flat(after)


def quarters(cells, parity, turn):
    q = cells.shape[-1] // 4
    a, b, c, d = (cells[..., i * q : (i + 1) * q] for i in range(4))
    even, odd = jnp.concatenate([a, c], axis=-1), jnp.concatenate([b, d], axis=-1)
    even_back, odd_back = jnp.concatenate([c, a], axis=-1), jnp.concatenate([d, b], axis=-1)
    even, odd = jnp.where(turn == 0, even, even_back), jnp.where(turn == 0, odd, odd_back)
    return jnp.where(parity == 0, even, odd), jnp.where(parity == 0, odd, even)


def by_low_bit(cells, count, turn):
    w = cells.shape[-1] // count
    even = jnp.concatenate([cells[..., j * w : (j + 1) * w] for j in range(0, count, 2)], axis=-1)
    odd = jnp.concatenate([cells[..., j * w : (j + 1) * w] for j in range(1, count, 2)], axis=-1)
    return jnp.concatenate([jnp.where(turn == 0, even, odd), jnp.where(turn == 0, odd, even)], axis=-1)


def store_edges(cells, ref_a, ref_b, at):
    width = cells.shape[1] // 2
    even = bit_of("seq", 0) == 0
    head, tail = cells[:, :width], cells[:, width:]
    ref_a[:, at : at + width] = jnp.where(even, tail, head)
    ref_b[:, at : at + width] = jnp.where(even, head, tail)


def halos(ref_a, ref_b, at, width):
    even = bit_of("seq", 0) == 0
    a, b = ref_a[:, at : at + width], ref_b[:, at : at + width]
    return jnp.where(even, b, a), jnp.where(even, a, b)


def edge_body(near, far, h_ref, q_ref, a_ref, b_ref):
    rows = h_ref.shape[1]
    q = jnp.concatenate([q_ref[:, :far], q_ref[:, rows - far :]], axis=1)
    h = jnp.concatenate([h_ref[:, :near], h_ref[:, rows - near :]], axis=1)
    store_edges(q, a_ref, b_ref, 0)
    store_edges(h, a_ref, b_ref, far)


def first_body(near, h_ref, w_ref, s_ref, z_ref):
    act, _, _ = normed(h_ref[...])
    s = gelu(act)
    edge = jnp.zeros((s.shape[0], near, s.shape[2]), F32)
    before, own, after = (v.astype(BF16) for v in windows(edge, s, edge))
    s_ref[...] = own.reshape(s_ref.shape)
    z = dot(own, w_ref[0, 1]) + dot(before, w_ref[0, 0]) + dot(after, w_ref[0, 2])
    z_ref[...] = z.reshape(z_ref.shape)


def second_body(near, far, z_ref, h_ref, s_ref, a_ref, b_ref, w_ref, h1_ref, s1_ref, keep_ref, send_ref, kx_ref, sx_ref, na_ref, nb_ref, ends_ref):
    rows = h_ref.shape[1]
    parity, turn = bit_of("dp", 0), bit_of("dp", 1)
    above, below = halos(a_ref, b_ref, far, near)
    above, below = gelu(normed(above)[0]), gelu(normed(below)[0])
    ext = jnp.concatenate([above, s_ref[...].astype(F32), below], axis=1).astype(BF16)
    ends_ref[:, :far], ends_ref[:, far:] = halos(a_ref, b_ref, 0, far)
    kx_ref[...], sx_ref[...] = quarters(ext, parity, turn)
    add_top = dot(flat(above).astype(BF16), w_ref[0, 0]).reshape(above.shape)
    add_low = dot(flat(below).astype(BF16), w_ref[0, 2]).reshape(below.shape)
    z = z_ref[...]
    z = jnp.concatenate([z[:, :near] + add_top, z[:, near : rows - near], z[:, rows - near :] + add_low], axis=1)
    h1 = (h_ref[...].astype(F32) + z).astype(BF16)
    h1_ref[...] = h1
    s1 = gelu(normed(h1)[0]).astype(BF16)
    s1_ref[...] = s1
    store_edges(jnp.concatenate([s1[:, :far], s1[:, rows - far :]], axis=1), na_ref, nb_ref, 0)
    keep_ref[...], send_ref[...] = quarters(s1, parity, turn)


def back_conv(layer, dtype, above, below, q, w_ref):
    before, own, after = windows(above.astype(dtype), q.astype(dtype), below.astype(dtype))
    e = dot_nt(own.astype(BF16), w_ref[layer, 1])
    e += dot_nt(after.astype(BF16), w_ref[layer, 0])
    return e + dot_nt(before.astype(BF16), w_ref[layer, 2])


def through_norm(e, h_ref, g):
    act, recip, wide = normed(h_ref[...])
    through = e.reshape(act.shape) * gelu_slope(act)
    inner = jnp.mean(through * wide, axis=-1, keepdims=True)
    return g + recip * through - wide * (recip * recip * recip * inner)


def back_inner_body(far, q_ref, w_ref, e_ref):
    edge = jnp.zeros((q_ref.shape[0], far, q_ref.shape[2]), BF16)
    e_ref[...] = back_conv(1, BF16, edge, edge, q_ref[...], w_ref).reshape(e_ref.shape)


def back_body(near, far, count, e_ref, q_ref, a_ref, b_ref, w_ref, h_ref, g_ref, out_ref, mixed_ref, na_ref, nb_ref):
    rows = q_ref.shape[1]
    above, below = halos(a_ref, b_ref, 0, far)
    top = e_ref[:, :far] + dot_nt(flat(above), w_ref[1, 2]).reshape(above.shape)
    low = e_ref[:, rows - far :] + dot_nt(flat(below), w_ref[1, 0]).reshape(below.shape)
    e = jnp.concatenate([top, e_ref[:, far : rows - far], low], axis=1)
    g = through_norm(e, h_ref, q_ref[...].astype(F32))
    g_ref[...] = g
    q = g.astype(BF16)
    out_ref[...] = q
    mixed_ref[...] = by_low_bit(q, count, bit_of("seq", 0))
    ends = jnp.concatenate([g[:, :near], g[:, rows - near :]], axis=1).astype(BF16)
    store_edges(ends, na_ref, nb_ref, 0)


def last_back_body(near, q_ref, a_ref, b_ref, w_ref, h_ref, g_ref, out_ref):
    above, below = halos(a_ref, b_ref, 0, near)
    e = back_conv(0, F32, above, below, q_ref[...], w_ref)
    out_ref[...] = through_norm(e, h_ref, g_ref[...]).astype(BF16)


def last_body(far, s_ref, a_ref, b_ref, w_ref, h_ref, out_ref):
    above, below = halos(a_ref, b_ref, 0, far)
    before, own, after = windows(above, s_ref[...], below)
    z = dot(before, w_ref[1, 0]) + dot(own, w_ref[1, 1]) + dot(after, w_ref[1, 2])
    out_ref[...] = (h_ref[...].astype(F32) + z.reshape(h_ref.shape)).astype(BF16)


def store_grad(tap, d, keep_ref, send_ref):
    tall, wide = d.shape[0] // 2, d.shape[1] // 2
    first = bit_of("dp", 0) == 0
    right, low = d[:tall, wide:], d[tall:, :wide]
    keep_ref[0, tap] = d[:tall, :wide]
    keep_ref[1, tap] = jnp.where(first, right, low)
    send_ref[0, tap] = jnp.where(first, low, right).astype(BF16)
    send_ref[1, tap] = d[tall:, wide:].astype(BF16)


def grad_near_body(s_ref, s2_ref, q_ref, q2_ref, keep_ref, send_ref):
    rows = q_ref.shape[1]
    step = (s_ref.shape[1] - rows) // 2
    q = jnp.concatenate([flat(q_ref[...]), flat(q2_ref[...])], axis=0)
    for tap in range(3):
        cut = slice(tap * step, tap * step + rows)
        s = jnp.concatenate([flat(s_ref[:, cut]), flat(s2_ref[:, cut])], axis=0)
        store_grad(tap, dot_tn(s, q), keep_ref, send_ref)


def grad_far_body(far, count, s_ref, s2_ref, q_ref, q2_ref, ends_ref, ends2_ref, keep_ref, send_ref):
    turn = bit_of("seq", 0)
    s = jnp.concatenate([flat(s_ref[...]), flat(s2_ref[...])], axis=0)
    taps = []
    for own_ref, at_ref in ((q_ref, ends_ref), (q2_ref, ends2_ref)):
        above, below = at_ref[:, :far], at_ref[:, far:]
        before, own, after = windows(*(by_low_bit(v, count, turn) for v in (above, own_ref[...], below)))
        taps.append((after, own, before))
    for tap in range(3):
        q = jnp.concatenate([taps[0][tap], taps[1][tap]], axis=0)
        store_grad(tap, dot_tn(s, q), keep_ref, send_ref)


def pass_body(keep_ref, got_ref, send_ref):
    for slot in range(send_ref.shape[0]):
        send_ref[slot] = (keep_ref[2 * slot + 1] + got_ref[2 * slot + 1].astype(F32)).astype(BF16)


def weave_body(count, keep_ref, got_ref, more_ref, out_ref, send_ref, all_ref):
    total = flat(keep_ref[0] + got_ref[0].astype(F32) + more_ref[0].astype(F32))
    w, r = total.shape[1] // count, total.shape[0] // count
    for block in range(count):
        all_ref[block] = jnp.concatenate(
            [total[g * r : (g + 1) * r, block * w : (block + 1) * w] for g in range(count)], axis=1
        )
    mine = lax.axis_index("seq") >> 1
    for slot in range(count // 2):
        out_ref[slot] = all_ref[mine ^ (3 * slot)]
        send_ref[slot] = all_ref[mine ^ 1 ^ (3 * slot)].astype(BF16)


def final_body(count, factor, *refs):
    out_ref = refs[-1]
    for layer in range(out_ref.shape[0]):
        keep_ref, got_ref, more_ref = refs[3 * layer : 3 * layer + 3]
        total = (keep_ref[0] + got_ref[0].astype(F32) + more_ref[0].astype(F32)) * factor
        w = total.shape[1] // count
        rows = jnp.concatenate([total[:, g * w : (g + 1) * w] for g in range(count)], axis=0)
        out_ref[layer] = rows.reshape(out_ref.shape[1:])


def per_device(embeddings, kernels, cotangent):
    batches, rows, channels = embeddings.shape
    seqs, dps = lax.axis_size("seq"), lax.axis_size("dp")
    near, far = FIRST_DILATION, 2 * FIRST_DILATION
    conv_flops = 6 * batches * rows * channels * channels
    half = channels // 2
    own = (batches, rows, channels)
    edges = (batches, near + far, channels)

    def paired(partner):
        pairs = []
        for s in range(seqs):
            for d in range(dps):
                t, e = partner(s, d)
                if 0 <= t < seqs:
                    pairs.append((s * dps + d, t * dps + e))
        return partial(lax.ppermute, axis_name=("seq", "dp"), perm=pairs)

    swap = paired(lambda s, d: (s, d ^ 1))
    to_a = paired(lambda s, d: (s ^ 1, d))
    to_b = paired(lambda s, d: (((s + 1) ^ 1) - 1, d))
    cross_one = paired(lambda s, d: (s, d ^ 2) if d % 2 == 0 else (s ^ 1, d))
    cross_two = paired(lambda s, d: (s ^ 1, d) if d % 2 == 0 else (s, d ^ 2))

    def along(bit):
        return paired(lambda s, d: (s ^ bit, d))

    send_a, send_b = kernel_call(
        partial(edge_body, near, far), [embeddings, cotangent], [shape(edges), shape(edges)]
    )
    got_a, got_b = to_a(send_a), to_b(send_b)
    q1_other = swap(cotangent)
    s0, z0 = kernel_call(
        partial(first_body, near), [embeddings, kernels], [shape(own), shape(own, F32)], conv_flops
    )
    (e1,) = kernel_call(
        partial(back_inner_body, far), [cotangent, kernels], [shape(own, F32)], conv_flops
    )
    h1, s1, s1_keep, s1_send, s0_keep, s0_send, s1_a, s1_b, ends = kernel_call(
        partial(second_body, near, far),
        [z0, embeddings, s0, got_a, got_b, kernels],
        [
            shape(own),
            shape(own),
            shape((batches, rows, half)),
            shape((batches, rows, half)),
            shape((batches, rows + 2 * near, half)),
            shape((batches, rows + 2 * near, half)),
            shape((batches, far, channels)),
            shape((batches, far, channels)),
            shape((batches, 2 * far, channels)),
        ],
        conv_flops // 10,
        [e1, q1_other],
    )
    ends_other, s1_other, s0_other = swap(ends), swap(s1_send), swap(s0_send)
    s1_a, s1_b = to_a(s1_a), to_b(s1_b)

    blocks = [shape((2, 3, half // 2, half), F32), shape((2, 3, half // 2, half))]
    count = seqs // 2
    strip = 3 * (half // 2) // count
    woven = strip % 16 == 0 and count <= 4
    factor = 1.0 / math.sqrt(batches * dps * rows * seqs)

    def passed(keep, got, after=()):
        sent = shape((keep.shape[0] // 2, *keep.shape[1:]))
        (send,) = kernel_call(pass_body, [keep, got], [sent], after=after)
        return send

    def reduced(keep, got, after=()):
        more = cross_two(passed(keep, got, after))
        if woven:
            keep, send, _ = kernel_call(
                partial(weave_body, count),
                [keep, got, more],
                [
                    shape((count // 2, strip, half), F32),
                    shape((count // 2, strip, half)),
                    shape((count, strip, half), F32),
                ],
            )
        else:
            total = keep[0] + got[0].astype(F32) + more[0].astype(F32)
            total = total.reshape(count, strip, count, half // count)
            total = total.transpose(2, 1, 0, 3).reshape(count, strip, half)
            total = total[jnp.arange(count) ^ (lax.axis_index("seq") // 2)]
            keep, send = total[0::2], total[1::2].astype(BF16)
        got, bit = along(2)(send), 4
        while 2 * bit < seqs:
            total = keep + got.astype(F32)
            keep, got, bit = total[0::2], along(bit)(total[1::2].astype(BF16)), 2 * bit
        if bit < seqs:
            return keep, got, along(bit + 2 if woven else bit)(passed(keep, got))
        return keep, got, jnp.zeros_like(got)

    g1, q0, q0_mixed, send_a, send_b = kernel_call(
        partial(back_body, near, far, seqs),
        [e1, cotangent, got_a, got_b, kernels, h1],
        [shape(own, F32), shape(own), shape(own)] + [shape((batches, near, channels))] * 2,
        conv_flops // 10,
        [s1_other, ends_other],
    )
    q0_a, q0_b = to_a(send_a), to_b(send_b)
    keep1, send1 = kernel_call(
        partial(grad_far_body, far, seqs),
        [s1_keep, s1_other, cotangent, q1_other, ends, ends_other],
        blocks,
        conv_flops,
        [g1],
    )
    half1 = cross_one(send1)

    q0_other = swap(q0_mixed)
    keep0, send0 = kernel_call(
        grad_near_body, [s0_keep, s0_other, q0_mixed, q0_other], blocks, conv_flops
    )
    half0 = cross_one(send0)
    parts1 = reduced(keep1, half1, [send0])
    parts0 = reduced(keep0, half0, [q0_a, q0_b, s1_a, s1_b])

    (out,) = kernel_call(
        partial(last_body, far), [s1, s1_a, s1_b, kernels, h1], [shape(own)], conv_flops
    )
    (grad_in,) = kernel_call(
        partial(last_back_body, near),
        [q0, q0_a, q0_b, kernels, embeddings, g1],
        [shape(own)],
        conv_flops,
    )
    final = (2, 3, half // 2, half // count)
    if woven:
        (grads,) = kernel_call(
            partial(final_body, count, factor), [*parts0, *parts1], [shape(final, F32)]
        )
        return out, grad_in, grads
    grads = []
    for keep, got, more in (parts0, parts1):
        total = (keep[0] + got[0].astype(F32) + more[0].astype(F32)) * factor
        grads.append(total.reshape(strip, count, half // count).transpose(1, 0, 2).reshape(final[1:]))
    return out, grad_in, jnp.stack(grads)


def solution(mesh):
    placed = (P("dp", "seq", None), P(), P("dp", "seq", None))
    return jax.shard_map(
        per_device,
        mesh=mesh,
        in_specs=placed,
        out_specs=(P("dp", "seq", None), P("dp", "seq", None), P(None, None, "dp", "seq")),
        check_vma=False,
    )
```

```python
import math
from functools import partial

import jax
import jax.numpy as jnp
from jax import lax
from jax.experimental import pallas as pl
from jax.experimental.pallas import tpu as pltpu
from jax.sharding import PartitionSpec as P

FIRST_DILATION = 8
F32 = jnp.float32
BF16 = jnp.bfloat16
VMEM = pl.BlockSpec(memory_space=pltpu.VMEM)
VMEM_LIMIT = 20 * 2**20
ROOT = math.sqrt(2.0 / math.pi)
CUBE = 0.044715


def kernel_call(body, args, outs, flops=0, after=()):
    if after:
        inner, first = body, len(args)
        body = lambda *refs: inner(*refs[:first], *refs[first + len(after) :])
    moved = sum(a.size * a.dtype.itemsize for a in args)
    moved += sum(math.prod(o.shape) * o.dtype.itemsize for o in outs)
    return pl.pallas_call(
        body,
        out_shape=tuple(outs),
        in_specs=[VMEM] * len(args) + [pl.BlockSpec(memory_space=pl.ANY)] * len(after),
        out_specs=tuple(VMEM for _ in outs),
        compiler_params=pltpu.CompilerParams(vmem_limit_bytes=VMEM_LIMIT),
        cost_estimate=pl.CostEstimate(flops=flops, bytes_accessed=moved, transcendentals=0),
    )(*args, *after)


def shape(dims, dtype=BF16):
    return jax.ShapeDtypeStruct(tuple(dims), dtype)


def bit_of(axis, bit):
    return (lax.axis_index(axis) >> bit) & 1


def normed(hidden):
    wide = hidden.astype(F32)
    recip = lax.rsqrt(jnp.mean(wide * wide, axis=-1, keepdims=True) + 1e-05)
    return wide * recip, recip, wide


def gelu(v):
    return 0.5 * v * (1.0 + jnp.tanh(ROOT * (v + CUBE * (v * v * v))))


def gelu_slope(v):
    square = v * v
    t = jnp.tanh(ROOT * v * (1.0 + CUBE * square))
    return 0.5 * (1.0 + t) + 0.5 * v * (1.0 - t * t) * (ROOT * (1.0 + 3.0 * CUBE * square))


def flat(cells):
    return cells.reshape(-1, cells.shape[-1])


def dot(a, b):
    return jnp.dot(a, b, preferred_element_type=F32)


def dot_nt(a, b):
    return lax.dot_general(a, b, (((1,), (1,)), ((), ())), preferred_element_type=F32)


def dot_tn(a, b):
    return lax.dot_general(a, b, (((0,), (0,)), ((), ())), preferred_element_type=F32)


def windows(above, own, below):
    width, rows = above.shape[1], own.shape[1]
    before = jnp.concatenate([above, own[:, : rows - width]], axis=1)
    after = jnp.concatenate([own[:, width:], below], axis=1)
    return flat(before), flat(own), flat(after)


def quarters(cells, parity, turn):
    q = cells.shape[-1] // 4
    a, b, c, d = (cells[..., i * q : (i + 1) * q] for i in range(4))
    even, odd = jnp.concatenate([a, c], axis=-1), jnp.concatenate([b, d], axis=-1)
    even_back, odd_back = jnp.concatenate([c, a], axis=-1), jnp.concatenate([d, b], axis=-1)
    even, odd = jnp.where(turn == 0, even, even_back), jnp.where(turn == 0, odd, odd_back)
    return jnp.where(parity == 0, even, odd), jnp.where(parity == 0, odd, even)


def by_low_bit(cells, count, turn):
    w = cells.shape[-1] // count
    even = jnp.concatenate([cells[..., j * w : (j + 1) * w] for j in range(0, count, 2)], axis=-1)
    odd = jnp.concatenate([cells[..., j * w : (j + 1) * w] for j in range(1, count, 2)], axis=-1)
    return jnp.concatenate([jnp.where(turn == 0, even, odd), jnp.where(turn == 0, odd, even)], axis=-1)


def store_edges(cells, ref_a, ref_b, at):
    width = cells.shape[1] // 2
    even = bit_of("seq", 0) == 0
    head, tail = cells[:, :width], cells[:, width:]
    ref_a[:, at : at + width] = jnp.where(even, tail, head)
    ref_b[:, at : at + width] = jnp.where(even, head, tail)


def halos(ref_a, ref_b, at, width):
    even = bit_of("seq", 0) == 0
    a, b = ref_a[:, at : at + width], ref_b[:, at : at + width]
    return jnp.where(even, b, a), jnp.where(even, a, b)


def edge_body(near, far, h_ref, q_ref, a_ref, b_ref):
    rows = h_ref.shape[1]
    q = jnp.concatenate([q_ref[:, :far], q_ref[:, rows - far :]], axis=1)
    h = jnp.concatenate([h_ref[:, :near], h_ref[:, rows - near :]], axis=1)
    store_edges(q, a_ref, b_ref, 0)
    store_edges(h, a_ref, b_ref, far)


def first_body(near, h_ref, w_ref, s_ref, z_ref):
    act, _, _ = normed(h_ref[...])
    s = gelu(act)
    edge = jnp.zeros((s.shape[0], near, s.shape[2]), F32)
    before, own, after = (v.astype(BF16) for v in windows(edge, s, edge))
    s_ref[...] = own.reshape(s_ref.shape)
    z = dot(own, w_ref[0, 1]) + dot(before, w_ref[0, 0]) + dot(after, w_ref[0, 2])
    z_ref[...] = z.reshape(z_ref.shape)


def second_body(near, far, z_ref, h_ref, s_ref, a_ref, b_ref, w_ref, h1_ref, s1_ref, keep_ref, send_ref, kx_ref, sx_ref, na_ref, nb_ref, ends_ref):
    rows = h_ref.shape[1]
    parity, turn = bit_of("dp", 0), bit_of("dp", 1)
    above, below = halos(a_ref, b_ref, far, near)
    above, below = gelu(normed(above)[0]), gelu(normed(below)[0])
    ext = jnp.concatenate([above, s_ref[...].astype(F32), below], axis=1).astype(BF16)
    ends_ref[:, :far], ends_ref[:, far:] = halos(a_ref, b_ref, 0, far)
    kx_ref[...], sx_ref[...] = quarters(ext, parity, turn)
    add_top = dot(flat(above).astype(BF16), w_ref[0, 0]).reshape(above.shape)
    add_low = dot(flat(below).astype(BF16), w_ref[0, 2]).reshape(below.shape)
    z = z_ref[...]
    z = jnp.concatenate([z[:, :near] + add_top, z[:, near : rows - near], z[:, rows - near :] + add_low], axis=1)
    h1 = (h_ref[...].astype(F32) + z).astype(BF16)
    h1_ref[...] = h1
    s1 = gelu(normed(h1)[0]).astype(BF16)
    s1_ref[...] = s1
    store_edges(jnp.concatenate([s1[:, :far], s1[:, rows - far :]], axis=1), na_ref, nb_ref, 0)
    keep_ref[...], send_ref[...] = quarters(s1, parity, turn)


def back_conv(layer, dtype, above, below, q, w_ref):
    before, own, after = windows(above.astype(dtype), q.astype(dtype), below.astype(dtype))
    e = dot_nt(own.astype(BF16), w_ref[layer, 1])
    e += dot_nt(after.astype(BF16), w_ref[layer, 0])
    return e + dot_nt(before.astype(BF16), w_ref[layer, 2])


def through_norm(e, h_ref, g):
    act, recip, wide = normed(h_ref[...])
    through = e.reshape(act.shape) * gelu_slope(act)
    inner = jnp.mean(through * wide, axis=-1, keepdims=True)
    return g + recip * through - wide * (recip * recip * recip * inner)


def back_inner_body(far, q_ref, w_ref, e_ref):
    edge = jnp.zeros((q_ref.shape[0], far, q_ref.shape[2]), BF16)
    e_ref[...] = back_conv(1, BF16, edge, edge, q_ref[...], w_ref).reshape(e_ref.shape)


def back_body(near, far, count, e_ref, q_ref, a_ref, b_ref, w_ref, h_ref, g_ref, out_ref, mixed_ref, na_ref, nb_ref):
    rows = q_ref.shape[1]
    above, below = halos(a_ref, b_ref, 0, far)
    top = e_ref[:, :far] + dot_nt(flat(above), w_ref[1, 2]).reshape(above.shape)
    low = e_ref[:, rows - far :] + dot_nt(flat(below), w_ref[1, 0]).reshape(below.shape)
    e = jnp.concatenate([top, e_ref[:, far : rows - far], low], axis=1)
    g = through_norm(e, h_ref, q_ref[...].astype(F32))
    g_ref[...] = g
    q = g.astype(BF16)
    out_ref[...] = q
    mixed_ref[...] = by_low_bit(q, count, bit_of("seq", 0))
    ends = jnp.concatenate([g[:, :near], g[:, rows - near :]], axis=1).astype(BF16)
    store_edges(ends, na_ref, nb_ref, 0)


def last_back_body(near, q_ref, a_ref, b_ref, w_ref, h_ref, g_ref, out_ref):
    above, below = halos(a_ref, b_ref, 0, near)
    e = back_conv(0, F32, above, below, q_ref[...], w_ref)
    out_ref[...] = through_norm(e, h_ref, g_ref[...]).astype(BF16)


def last_body(far, s_ref, a_ref, b_ref, w_ref, h_ref, out_ref):
    above, below = halos(a_ref, b_ref, 0, far)
    before, own, after = windows(above, s_ref[...], below)
    z = dot(before, w_ref[1, 0]) + dot(own, w_ref[1, 1]) + dot(after, w_ref[1, 2])
    out_ref[...] = (h_ref[...].astype(F32) + z.reshape(h_ref.shape)).astype(BF16)


def store_grad(tap, d, keep_ref, send_ref):
    tall, wide = d.shape[0] // 2, d.shape[1] // 2
    first = bit_of("dp", 0) == 0
    right, low = d[:tall, wide:], d[tall:, :wide]
    keep_ref[0, tap] = d[:tall, :wide]
    keep_ref[1, tap] = jnp.where(first, right, low)
    send_ref[0, tap] = jnp.where(first, low, right).astype(BF16)
    send_ref[1, tap] = d[tall:, wide:].astype(BF16)


def grad_near_body(s_ref, s2_ref, q_ref, q2_ref, keep_ref, send_ref):
    rows = q_ref.shape[1]
    step = (s_ref.shape[1] - rows) // 2
    q = jnp.concatenate([flat(q_ref[...]), flat(q2_ref[...])], axis=0)
    for tap in range(3):
        cut = slice(tap * step, tap * step + rows)
        s = jnp.concatenate([flat(s_ref[:, cut]), flat(s2_ref[:, cut])], axis=0)
        store_grad(tap, dot_tn(s, q), keep_ref, send_ref)


def grad_far_body(far, count, s_ref, s2_ref, q_ref, q2_ref, ends_ref, ends2_ref, keep_ref, send_ref):
    turn = bit_of("seq", 0)
    s = jnp.concatenate([flat(s_ref[...]), flat(s2_ref[...])], axis=0)
    taps = []
    for own_ref, at_ref in ((q_ref, ends_ref), (q2_ref, ends2_ref)):
        above, below = at_ref[:, :far], at_ref[:, far:]
        before, own, after = windows(*(by_low_bit(v, count, turn) for v in (above, own_ref[...], below)))
        taps.append((after, own, before))
    for tap in range(3):
        q = jnp.concatenate([taps[0][tap], taps[1][tap]], axis=0)
        store_grad(tap, dot_tn(s, q), keep_ref, send_ref)


def pass_body(keep_ref, got_ref, send_ref):
    for slot in range(send_ref.shape[0]):
        send_ref[slot] = (keep_ref[2 * slot + 1] + got_ref[2 * slot + 1].astype(F32)).astype(BF16)


def weave_body(count, keep_ref, got_ref, more_ref, out_ref, send_ref, all_ref):
    total = flat(keep_ref[0] + got_ref[0].astype(F32) + more_ref[0].astype(F32))
    w, r = total.shape[1] // count, total.shape[0] // count
    for block in range(count):
        all_ref[block] = jnp.concatenate(
            [total[g * r : (g + 1) * r, block * w : (block + 1) * w] for g in range(count)], axis=1
        )
    mine = lax.axis_index("seq") >> 1
    for slot in range(count // 2):
        out_ref[slot] = all_ref[mine ^ (3 * slot)]
        send_ref[slot] = all_ref[mine ^ 1 ^ (3 * slot)].astype(BF16)


def final_body(count, factor, *refs):
    out_ref = refs[-1]
    for layer in range(out_ref.shape[0]):
        keep_ref, got_ref, more_ref = refs[3 * layer : 3 * layer + 3]
        total = (keep_ref[0] + got_ref[0].astype(F32) + more_ref[0].astype(F32)) * factor
        w = total.shape[1] // count
        rows = jnp.concatenate([total[:, g * w : (g + 1) * w] for g in range(count)], axis=0)
        out_ref[layer] = rows.reshape(out_ref.shape[1:])


def per_device(embeddings, kernels, cotangent):
    batches, rows, channels = embeddings.shape
    seqs, dps = lax.axis_size("seq"), lax.axis_size("dp")
    near, far = FIRST_DILATION, 2 * FIRST_DILATION
    conv_flops = 6 * batches * rows * channels * channels
    half = channels // 2
    own = (batches, rows, channels)
    edges = (batches, near + far, channels)

    def paired(partner):
        pairs = []
        for s in range(seqs):
            for d in range(dps):
                t, e = partner(s, d)
                if 0 <= t < seqs:
                    pairs.append((s * dps + d, t * dps + e))
        return partial(lax.ppermute, axis_name=("seq", "dp"), perm=pairs)

    swap = paired(lambda s, d: (s, d ^ 1))
    to_a = paired(lambda s, d: (s ^ 1, d))
    to_b = paired(lambda s, d: (((s + 1) ^ 1) - 1, d))
    cross_one = paired(lambda s, d: (s, d ^ 2) if d % 2 == 0 else (s ^ 1, d))
    cross_two = paired(lambda s, d: (s ^ 1, d) if d % 2 == 0 else (s, d ^ 2))

    def along(bit):
        return paired(lambda s, d: (s ^ bit, d))

    send_a, send_b = kernel_call(
        partial(edge_body, near, far), [embeddings, cotangent], [shape(edges), shape(edges)]
    )
    got_a, got_b = to_a(send_a), to_b(send_b)
    q1_other = swap(cotangent)
    s0, z0 = kernel_call(
        partial(first_body, near), [embeddings, kernels], [shape(own), shape(own, F32)], conv_flops
    )
    (e1,) = kernel_call(
        partial(back_inner_body, far), [cotangent, kernels], [shape(own, F32)], conv_flops
    )
    h1, s1, s1_keep, s1_send, s0_keep, s0_send, s1_a, s1_b, ends = kernel_call(
        partial(second_body, near, far),
        [z0, embeddings, s0, got_a, got_b, kernels],
        [
            shape(own),
            shape(own),
            shape((batches, rows, half)),
            shape((batches, rows, half)),
            shape((batches, rows + 2 * near, half)),
            shape((batches, rows + 2 * near, half)),
            shape((batches, far, channels)),
            shape((batches, far, channels)),
            shape((batches, 2 * far, channels)),
        ],
        conv_flops // 10,
        [e1, q1_other],
    )
    ends_other, s1_other, s0_other = swap(ends), swap(s1_send), swap(s0_send)
    s1_a, s1_b = to_a(s1_a), to_b(s1_b)

    blocks = [shape((2, 3, half // 2, half), F32), shape((2, 3, half // 2, half))]
    count = seqs // 2
    strip = 3 * (half // 2) // count
    woven = strip % 16 == 0 and count <= 4
    factor = 1.0 / math.sqrt(batches * dps * rows * seqs)

    def passed(keep, got, after=()):
        sent = shape((keep.shape[0] // 2, *keep.shape[1:]))
        (send,) = kernel_call(pass_body, [keep, got], [sent], after=after)
        return send

    def reduced(keep, got, after=()):
        more = cross_two(passed(keep, got, after))
        if woven:
            keep, send, _ = kernel_call(
                partial(weave_body, count),
                [keep, got, more],
                [
                    shape((count // 2, strip, half), F32),
                    shape((count // 2, strip, half)),
                    shape((count, strip, half), F32),
                ],
            )
        else:
            total = keep[0] + got[0].astype(F32) + more[0].astype(F32)
            total = total.reshape(count, strip, count, half // count)
            total = total.transpose(2, 1, 0, 3).reshape(count, strip, half)
            total = total[jnp.arange(count) ^ (lax.axis_index("seq") // 2)]
            keep, send = total[0::2], total[1::2].astype(BF16)
        got, bit = along(2)(send), 4
        while 2 * bit < seqs:
            total = keep + got.astype(F32)
            keep, got, bit = total[0::2], along(bit)(total[1::2].astype(BF16)), 2 * bit
        if bit < seqs:
            return keep, got, along(bit + 2 if woven else bit)(passed(keep, got))
        return keep, got, jnp.zeros_like(got)

    g1, q0, q0_mixed, send_a, send_b = kernel_call(
        partial(back_body, near, far, seqs),
        [e1, cotangent, got_a, got_b, kernels, h1],
        [shape(own, F32), shape(own), shape(own)] + [shape((batches, near, channels))] * 2,
        conv_flops // 10,
        [s1_other, ends_other],
    )
    q0_a, q0_b = to_a(send_a), to_b(send_b)
    keep1, send1 = kernel_call(
        partial(grad_far_body, far, seqs),
        [s1_keep, s1_other, cotangent, q1_other, ends, ends_other],
        blocks,
        conv_flops,
        [g1],
    )
    half1 = cross_one(send1)

    q0_other = swap(q0_mixed)
    keep0, send0 = kernel_call(
        grad_near_body, [s0_keep, s0_other, q0_mixed, q0_other], blocks, conv_flops
    )
    half0 = cross_one(send0)
    parts1 = reduced(keep1, half1, [send0])
    parts0 = reduced(keep0, half0)

    (out,) = kernel_call(
        partial(last_body, far), [s1, s1_a, s1_b, kernels, h1], [shape(own)], conv_flops
    )
    (grad_in,) = kernel_call(
        partial(last_back_body, near),
        [q0, q0_a, q0_b, kernels, embeddings, g1],
        [shape(own)],
        conv_flops,
    )
    final = (2, 3, half // 2, half // count)
    if woven:
        (grads,) = kernel_call(
            partial(final_body, count, factor), [*parts0, *parts1], [shape(final, F32)]
        )
        return out, grad_in, grads
    grads = []
    for keep, got, more in (parts0, parts1):
        total = (keep[0] + got[0].astype(F32) + more[0].astype(F32)) * factor
        grads.append(total.reshape(strip, count, half // count).transpose(1, 0, 2).reshape(final[1:]))
    return out, grad_in, jnp.stack(grads)


def solution(mesh):
    placed = (P("dp", "seq", None), P(), P("dp", "seq", None))
    return jax.shard_map(
        per_device,
        mesh=mesh,
        in_specs=placed,
        out_specs=(P("dp", "seq", None), P("dp", "seq", None), P(None, None, "dp", "seq")),
        check_vma=False,
    )
```
